32 devices in a mesh: rows: 16 (over z, y, x), cols: 2 (over core).
Axes of the slice: x: 2, y: 2, z: 4, core: 2. Of those that a mesh axis runs over, the one named last changes fastest.
Arguments:
- pair_map: bfloat16 [32, 128, 2048], P(None, 'cols', 'rows'), may hold values from -44 to 44
- conv_in: bfloat16 [32, 288], replicated, may hold values from -0.375 to 0.375
- embed_weight: bfloat16 [2048, 256], replicated, may hold values from -0.125 to 0.125
- qkv_weight: bfloat16 [256, 768], replicated, may hold values from -0.5 to 0.5
- key_bias: bfloat16 [256, 16, 8], P('rows', 'cols'), may hold values from -4 to 260
- out_weight: bfloat16 [256, 256], replicated, may hold values from -0.375 to 0.375
- unpatch: bfloat16 [256, 2048], replicated, may hold values from -0.375 to 0.375
- conv_out: bfloat16 [32, 288], replicated, may hold values from -0.375 to 0.375
Outputs:
- trunk_out: bfloat16 [32, 128, 2048], P(None, 'cols', 'rows')
The draws below stay inside these ranges and needn't reach their ends.
All inputs are finite; a program needn't handle non-finite values.
Results may differ from the reference program's by a relative error of at most 0.014.
Values may be sent and summed in bfloat16 or wider, within the bound.
A program may use at most 128 MiB of HBM per device.

```python
import jax
import jax.numpy as jnp
from jax import lax

C = 32
PATCH = 8
D = 256
HEADS = 8
HEAD_DIM = 32
ROWS_DEV = 128
COLS_DEV = 64
LENGTH = 2048
SLAB = 128
PROWS = 256
PCOLS = 16


def draw_pair_map(key, part):
    base_key = jax.random.fold_in(key, 23)
    map_shape = (C, SLAB, LENGTH)
    col_place = jnp.arange(SLAB) % COLS_DEV
    row_place = jnp.arange(LENGTH) % ROWS_DEV
    col_edge = jnp.logical_or(col_place == 0, col_place == COLS_DEV - 1)
    row_edge = jnp.logical_or(row_place == 0, row_place == ROWS_DEV - 1)
    corner = jnp.logical_and(col_edge[:, None], row_edge[None, :])[None, :, :]
    spread = jnp.clip(jax.random.normal(base_key, map_shape, jnp.float32), -6.0, 6.0)
    peak = jnp.where(spread >= 0.0, 1.0, -1.0) * (28.0 + 4.0 * jnp.minimum(jnp.abs(spread), 4.0))
    return jnp.where(corner, peak, spread).astype(jnp.bfloat16)


def draw_key_bias(key, part):
    base_key = jax.random.fold_in(key, 11)
    key_list = jax.random.split(base_key, 5)
    bias_shape = (PROWS, PCOLS, HEADS)
    pair_count = PCOLS * HEADS
    row_index = jnp.arange(PROWS)[:, None]
    background = jax.random.uniform(key_list[0], (PROWS, pair_count), jnp.float32, 0.0, 0.9)
    spike_row = jax.random.randint(key_list[4], (pair_count,), 0, PROWS)
    values = jnp.where(row_index == spike_row[None, :], 8.0, background)
    return values.reshape(bias_shape).astype(jnp.bfloat16)


def noise(key, dims, width, bound, dtype=jnp.bfloat16):
    entries = jax.random.normal(key, dims, jnp.float32) * width
    return jnp.minimum(jnp.maximum(entries, -bound), bound).astype(dtype)


def setup_inputs(seed: int = 0) -> dict:
    key_of = jax.random.split(jax.random.key(seed), 9)
    pair_map = draw_pair_map(jax.random.fold_in(key_of[8], 71), 0)
    conv_in = noise(key_of[1], (C, 9 * C), (9 * C) ** -0.5, 0.375)
    embed_weight = noise(key_of[2], (C * PATCH * PATCH, D), (C * PATCH * PATCH) ** -0.5, 0.125)
    qkv_weight = noise(key_of[3], (D, 3 * D), (D // 2) ** -0.5, 0.5)
    key_bias = draw_key_bias(jax.random.fold_in(key_of[8], 71), 0)
    out_weight = noise(key_of[5], (D, D), D ** -0.5, 0.375)
    unpatch = noise(key_of[6], (D, C * PATCH * PATCH), D ** -0.5, 0.375)
    conv_out = noise(key_of[7], (C, 9 * C), (9 * C) ** -0.5, 0.375)
    return dict(pair_map=pair_map, conv_in=conv_in, embed_weight=embed_weight, qkv_weight=qkv_weight, key_bias=key_bias, out_weight=out_weight, unpatch=unpatch, conv_out=conv_out)


epsilon = 1e-05

def convolve(source_map, weight):
    kernel = weight.astype(jnp.float32).reshape(C, 3, 3, C).transpose(0, 3, 1, 2)
    result = lax.conv_general_dilated(source_map.astype(jnp.float32)[None], kernel, (1, 1), ((1, 1), (1, 1)), dimension_numbers=('NCHW', 'OIHW', 'NCHW'), precision=lax.Precision.HIGHEST)
    return result[0]

def layer_norm(tokens):
    values = tokens.astype(jnp.float32)
    row_mean = lax.optimization_barrier(jnp.mean(values, axis=1, keepdims=True))
    centered = values - row_mean
    row_var = lax.optimization_barrier(jnp.mean(centered * centered, axis=1, keepdims=True))
    return (centered * lax.rsqrt(row_var + epsilon)).astype(jnp.bfloat16)

def attend(qkv_rows, bias_row):
    seq_length = qkv_rows.shape[0]
    block_rows = min(512, seq_length)
    queries = qkv_rows[:, :HEAD_DIM]
    key_rows = qkv_rows[:, HEAD_DIM:2 * HEAD_DIM]
    value_rows = qkv_rows[:, 2 * HEAD_DIM:]
    key_shift = bias_row.astype(jnp.float32)[None, :]
    score_scale = HEAD_DIM ** (-0.5)

    def one_block(query_block):
        scores = jnp.dot(query_block, key_rows.T, preferred_element_type=jnp.float32) * score_scale + key_shift
        row_peak = lax.optimization_barrier(jnp.max(scores, axis=1, keepdims=True))
        weights = jnp.exp(scores - row_peak)
        soft_weights = (weights / lax.optimization_barrier(jnp.sum(weights, axis=1, keepdims=True))).astype(jnp.bfloat16)
        return jnp.dot(soft_weights, value_rows, preferred_element_type=jnp.float32).astype(jnp.bfloat16)
    result = lax.map(one_block, queries.reshape(seq_length // block_rows, block_rows, HEAD_DIM))
    return result.reshape(seq_length, HEAD_DIM)

def attend_pair(pair_item):
    return attend(pair_item[0], pair_item[1])

def reference(pair_map, conv_in, embed_weight, qkv_weight, key_bias, out_weight, unpatch, conv_out):
    first_conv = convolve(pair_map, conv_in)
    mixed_map = (pair_map.astype(jnp.float32) + jax.nn.silu(first_conv)).astype(jnp.bfloat16)
    patches = mixed_map.reshape(C, PCOLS, PATCH, PROWS, PATCH).transpose(3, 1, 0, 2, 4).reshape(PROWS * PCOLS, C * PATCH * PATCH)
    tokens = jnp.dot(patches, embed_weight, preferred_element_type=jnp.float32).astype(jnp.bfloat16)
    normed = layer_norm(tokens)
    projected = jnp.dot(normed, qkv_weight, preferred_element_type=jnp.float32).astype(jnp.bfloat16)
    pair_items = projected.reshape(PROWS, PCOLS, 3, HEADS, HEAD_DIM).transpose(1, 3, 0, 2, 4).reshape(PCOLS * HEADS, PROWS, 3 * HEAD_DIM)
    biases = key_bias.transpose(1, 2, 0).reshape(PCOLS * HEADS, PROWS)
    attended = lax.map(attend_pair, (pair_items, biases))
    attended = attended.reshape(PCOLS, HEADS, PROWS, HEAD_DIM).transpose(2, 0, 1, 3).reshape(PROWS * PCOLS, D)
    updated = (tokens.astype(jnp.float32) + jnp.dot(attended, out_weight, preferred_element_type=jnp.float32)).astype(jnp.bfloat16)
    expanded = jnp.dot(updated, unpatch, preferred_element_type=jnp.float32)
    expanded = expanded.reshape(PROWS, PCOLS, C, PATCH, PATCH).transpose(2, 1, 3, 0, 4).reshape(C, SLAB, LENGTH)
    merged = (mixed_map.astype(jnp.float32) + expanded).astype(jnp.bfloat16)
    second_conv = convolve(merged, conv_out)
    return (merged.astype(jnp.float32) + second_conv).astype(jnp.bfloat16)
```

```python
import functools

import jax
import jax.numpy as jnp
from jax import lax
from jax.experimental import pallas as pl
from jax.experimental.pallas import tpu as pltpu
from jax.sharding import PartitionSpec as P

C = 32
PATCH = 8
D = 256
HEADS = 8
HEAD_DIM = 32
LANES = 128
EPSILON = 1e-05
F32 = jnp.float32
BF16 = jnp.bfloat16
MESH = pl.DeviceIdType.MESH
NT = (((1,), (1,)), ((), ()))
TOP = 8


def dot(a, b):
    return jnp.dot(a, b, preferred_element_type=F32)


def dot_nt(a, b):
    return lax.dot_general(a, b, NT, preferred_element_type=F32)


def iota(shape, dim):
    return lax.broadcasted_iota(jnp.int32, shape, dim)


def trunk_kernel(
    R,
    NC,
    x_ref,
    kb_ref,
    cin_ref,
    cout_ref,
    embed_hbm,
    qkv_hbm,
    outw_hbm,
    unp_hbm,
    o_ref,
    tmap,
    mixed,
    edges,
    halo,
    wide,
    embed_v,
    qkv_v,
    outw_v,
    unp_v,
    embed_i,
    unp_i,
    taps,
    sendq,
    recvq,
    sendb,
    recvb,
    sendo,
    recvo,
    load_sem,
    halo_ss,
    halo_rs,
    col_ss,
    col_rs,
    q_ss,
    q_rs,
    b_ss,
    b_rs,
    o_ss,
    o_rs,
):
    row = lax.axis_index("rows")
    col = lax.axis_index("cols")
    NP = x_ref.shape[1] // PATCH
    L = x_ref.shape[2]
    PR = L // PATCH
    CJ = C * PATCH
    groups = NP * (D // LANES)
    split = R // groups
    group_heads = LANES // HEAD_DIM
    my_heads = group_heads // split
    keys = R * PR

    loads = [
        pltpu.make_async_copy(src, dst, load_sem.at[n])
        for n, (src, dst) in enumerate(
            ((embed_hbm, embed_v), (qkv_hbm, qkv_v), (outw_hbm, outw_v), (unp_hbm, unp_v))
        )
    ]
    for copy in loads:
        copy.start()

    row_ok = {-1: row > 0, 1: row < R - 1}
    col_ok = {-1: col > 0, 0: col >= 0, 1: col < NC - 1}
    barrier = pltpu.get_barrier_semaphore()

    def greet(d, carry):
        pl.semaphore_signal(
            barrier,
            inc=1,
            device_id={"rows": lax.rem(row + d, R), "cols": col},
            device_id_type=MESH,
        )
        return carry

    lax.fori_loop(1, R, greet, 0)
    expected = R - 1
    for dc in (-1, 1):
        for dr in (-1, 0, 1):
            ok = col_ok[dc] if dr == 0 else jnp.logical_and(col_ok[dc], row_ok[dr])
            expected = expected + ok.astype(jnp.int32)

            @pl.when(ok)
            def _():
                pl.semaphore_signal(
                    barrier,
                    inc=1,
                    device_id={"rows": row + dr, "cols": col + dc},
                    device_id_type=MESH,
                )

    def put_edges(phase):
        for p in range(NP):
            edges[phase, 0, p : p + 1, :] = tmap[phase, p + 1, TOP + L - 1 : TOP + L, :]
            edges[phase, 1, p : p + 1, :] = tmap[phase, p + 1, TOP : TOP + 1, :]

    for q in range(NP // 2):
        pair = x_ref[:, 2 * PATCH * q : 2 * PATCH * (q + 1), :].astype(F32)
        for s in range(2):
            block = pair[:, PATCH * s : PATCH * (s + 1), :].reshape(CJ, L)
            tmap[0, 1 + 2 * q + s, TOP : TOP + L, :] = block.T
    put_edges(0)

    bias = kb_ref[...].astype(F32)
    for p in range(NP):
        block = jnp.concatenate(
            [bias[:, p, :], jnp.zeros((PR, LANES - HEADS), F32)], axis=1
        )
        sendb[p] = block.astype(BF16)

    for phase in range(2):
        for way, dr in ((0, -1), (1, 1)):
            for slot in range(3):
                missing = jnp.logical_not(jnp.logical_and(row_ok[dr], col_ok[slot - 1]))

                @pl.when(missing)
                def _():
                    halo[phase, way, slot] = jnp.zeros((NP, CJ), F32)

        for side, dc in ((0, -1), (1, 1)):

            @pl.when(jnp.logical_not(col_ok[dc]))
            def _():
                tmap[phase, side * (NP + 1), TOP : TOP + L, :] = jnp.zeros((L, CJ), F32)

    pl.semaphore_wait(barrier, expected)

    def halo_copies(phase, act):
        for side, dc in ((0, 1), (1, -1)):
            copy = pltpu.make_async_remote_copy(
                src_ref=tmap.at[phase, NP if side == 0 else 1, pl.ds(TOP, L)],
                dst_ref=tmap.at[phase, 0 if side == 0 else NP + 1, pl.ds(TOP, L)],
                send_sem=col_ss.at[phase, side],
                recv_sem=col_rs.at[phase, side],
                device_id={"rows": row, "cols": col + (-dc if act == "recv" else dc)},
                device_id_type=MESH,
            )
            ok = col_ok[-dc] if act == "recv" else col_ok[dc]

            @pl.when(ok)
            def _():
                if act == "start":
                    copy.start()
                elif act == "send":
                    copy.wait_send()
                else:
                    copy.wait_recv()

        for way, dr in ((0, 1), (1, -1)):
            for slot in range(3):
                dc = slot - 1
                if act == "recv":
                    ok = jnp.logical_and(row_ok[-dr], col_ok[dc])
                    peer = {"rows": row - dr, "cols": col + dc}
                else:
                    ok = jnp.logical_and(row_ok[dr], col_ok[-dc])
                    peer = {"rows": row + dr, "cols": col - dc}
                copy = pltpu.make_async_remote_copy(
                    src_ref=edges.at[phase, way],
                    dst_ref=halo.at[phase, way, slot],
                    send_sem=halo_ss.at[phase, way, slot],
                    recv_sem=halo_rs.at[phase, way, slot],
                    device_id=peer,
                    device_id_type=MESH,
                )

                @pl.when(ok)
                def _():
                    if act == "start":
                        copy.start()
                    elif act == "send":
                        copy.wait_send()
                    else:
                        copy.wait_recv()

    def exchange(act, source, target, send_sem, recv_sem):
        def step(d, carry):
            peer = lax.rem(row + d, R)
            copy = pltpu.make_async_remote_copy(
                src_ref=source(peer),
                dst_ref=target.at[peer if act == "recv" else row],
                send_sem=send_sem.at[peer],
                recv_sem=recv_sem.at[peer if act == "recv" else row],
                device_id={"rows": peer, "cols": col},
                device_id_type=MESH,
            )
            if act == "start":
                copy.start()
            elif act == "send":
                copy.wait_send()
            else:
                copy.wait_recv()
            return carry

        lax.fori_loop(1, R, step, 0)

    halo_copies(0, "start")
    heads_per_col = split * (D // LANES)
    bias_source = lambda peer: sendb.at[peer // heads_per_col]
    exchange("start", bias_source, recvb, b_ss, b_rs)
    recvb[row] = sendb[row // heads_per_col]

    spread = (iota((CJ, C), 0) // PATCH == iota((CJ, C), 1)).astype(F32).astype(BF16)
    both = jnp.concatenate(
        [dot(spread, cin_ref[...]).astype(BF16), dot(spread, cout_ref[...]).astype(BF16)], axis=0
    )
    in_place = iota((CJ, 2 * CJ), 0) % PATCH
    out_place = iota((CJ, 2 * CJ), 1) % PATCH
    channel = iota((CJ, 9 * C), 0) // PATCH
    tap = iota((CJ, 9 * C), 1)
    for b in range(3):
        centre = jnp.zeros((CJ, 2 * CJ), F32)
        rim = jnp.zeros((CJ, 2 * CJ), F32)
        for a in range(3):
            pick = (tap == channel + (3 * a + b) * C).astype(F32).astype(BF16)
            full = dot_nt(pick, both)
            centre = jnp.where(in_place == out_place + (a - 1), full, centre)
            if a == 0:
                rim = jnp.where(in_place == out_place + (PATCH - 1), full, rim)
            if a == 2:
                rim = jnp.where(in_place == out_place - (PATCH - 1), full, rim)
        for n in range(2):
            taps[n, b, 0:CJ, :] = centre[:, n * CJ : (n + 1) * CJ].astype(BF16)
            taps[n, b, CJ : 2 * CJ, :] = rim[:, n * CJ : (n + 1) * CJ].astype(BF16)

    loads[0].wait()
    for half in range(2):
        wide[half] = embed_v[:, half * LANES : (half + 1) * LANES].astype(F32)
    for i in range(PATCH):
        for half in range(2):
            embed_i[i, :, half * LANES : (half + 1) * LANES] = wide[
                half, pl.ds(i, CJ, stride=PATCH), :
            ].astype(BF16)

    lane_place = iota((1, 1, CJ), 2) % PATCH

    def conv(phase):
        halo_copies(phase, "recv")
        for way, place in ((0, TOP - 1), (1, TOP + L)):
            for p in range(NP):
                tmap[phase, p + 1, place : place + 1, :] = halo[phase, way, 1, p : p + 1, :]
            tmap[phase, 0, place : place + 1, :] = halo[phase, way, 0, NP - 1 : NP, :]
            tmap[phase, NP + 1, place : place + 1, :] = halo[phase, way, 2, 0:1, :]
        total = None
        for b in range(3):
            cells = tmap[phase, :, TOP - 1 + b : TOP - 1 + b + L, :]
            centre = cells[1 : NP + 1].reshape(NP * L, CJ).astype(BF16)
            rim = jnp.where(
                lane_place == PATCH - 1,
                cells[0:NP],
                jnp.where(lane_place == 0, cells[2 : NP + 2], 0.0),
            )
            rim = rim.reshape(NP * L, CJ).astype(BF16)
            part = dot(centre, taps[phase, b, 0:CJ, :]) + dot(rim, taps[phase, b, CJ : 2 * CJ, :])
            total = part if total is None else total + part
        return total

    first = conv(0)
    base = tmap[0, 1 : NP + 1, TOP : TOP + L, :].reshape(NP * L, CJ)
    mix = (base + first / (1.0 + jnp.exp(-first))).astype(BF16).astype(F32)
    for half in range(2):
        mixed[half] = mix[:, half * LANES : (half + 1) * LANES]

    total = None
    for i in range(PATCH):
        for half in range(2):
            cells = mixed[half, pl.ds(i, NP * PR, stride=PATCH), :].astype(BF16)
            part = dot(cells, embed_i[i, half * LANES : (half + 1) * LANES, :])
            total = part if total is None else total + part
    tokens = total.astype(BF16).astype(F32)
    mean = jnp.mean(tokens, axis=1, keepdims=True)
    centred = tokens - mean
    var = jnp.mean(centred * centred, axis=1, keepdims=True)
    normed = (centred * lax.rsqrt(var + EPSILON)).astype(BF16)
    loads[1].wait()
    projected = dot(normed, qkv_v[...]).astype(BF16)
    for g in range(D // LANES):
        for kind in range(3):
            start = kind * D + g * LANES
            part = projected[:, start : start + LANES].reshape(NP, PR, LANES)
            for p in range(NP):
                sendq[p * (D // LANES) + g, :, kind * LANES : (kind + 1) * LANES] = part[p]
    q_source = lambda peer: sendq.at[peer // split]
    exchange("start", q_source, recvq, q_ss, q_rs)
    recvq[row] = sendq[row // split]

    loads[3].wait()
    for k in range(PATCH):
        block = unp_v[:, k * CJ : (k + 1) * CJ].astype(F32).T
        for half in range(2):
            wide[half, k * CJ : (k + 1) * CJ, :] = block[:, half * LANES : (half + 1) * LANES]
    for i in range(PATCH):
        for half in range(2):
            unp_i[i, :, half * LANES : (half + 1) * LANES] = wide[
                half, pl.ds(i, CJ, stride=PATCH), :
            ].astype(BF16)

    exchange("recv", bias_source, recvb, b_ss, b_rs)
    first_head = lax.rem(row, split) * my_heads
    first_global = lax.rem(row // split, D // LANES) * group_heads + first_head
    pick = (iota((16, LANES), 1) == iota((16, LANES), 0) + first_global).astype(F32).astype(BF16)
    key_shift = dot_nt(pick, recvb[...].reshape(keys, LANES))
    exchange("recv", q_source, recvq, q_ss, q_rs)
    queries = recvq[:, :, 0:LANES].reshape(keys, LANES).astype(F32)
    key_rows = recvq[:, :, LANES : 2 * LANES].reshape(keys, LANES)
    values = recvq[:, :, 2 * LANES : 3 * LANES].reshape(keys, LANES).astype(F32)
    lane_head = iota((1, LANES), 1) // HEAD_DIM
    total = None
    for k in range(my_heads):
        mine = lane_head == first_head + k
        query = jnp.where(mine, queries, 0.0).astype(BF16)
        scores = dot_nt(query, key_rows) * (HEAD_DIM**-0.5) + key_shift[k : k + 1, :]
        weights = jnp.exp(scores - jnp.max(scores, axis=1, keepdims=True))
        soft = (weights / jnp.sum(weights, axis=1, keepdims=True)).astype(BF16)
        part = dot(soft, jnp.where(mine, values, 0.0).astype(BF16))
        total = part if total is None else total + part
    sendo[...] = total.astype(BF16).reshape(R, PR, LANES)
    o_source = lambda peer: sendo.at[peer]
    exchange("start", o_source, recvo, o_ss, o_rs)
    recvo[row] = sendo[row]
    loads[2].wait()
    exchange("send", bias_source, recvb, b_ss, b_rs)
    exchange("send", q_source, recvq, q_ss, q_rs)
    halo_copies(0, "send")
    exchange("recv", o_source, recvo, o_ss, o_rs)

    back = recvo[...].reshape(NP, D // LANES, split, PR, LANES)
    sides = []
    for g in range(D // LANES):
        share = back[:, g, 0]
        for s in range(1, split):
            share = share + back[:, g, s]
        sides.append(share.reshape(NP * PR, LANES))
    attended = jnp.concatenate(sides, axis=1)
    updated = (tokens + dot(attended, outw_v[...])).astype(BF16)
    for i in range(PATCH):
        expanded = dot_nt(updated, unp_i[i])
        for half in range(2):
            wide[half, pl.ds(i, NP * PR, stride=PATCH), :] = expanded[
                :, half * LANES : (half + 1) * LANES
            ]
    merged = jnp.concatenate(
        [mixed[half] + wide[half, 0 : NP * L, :] for half in range(2)], axis=1
    )
    merged = merged.astype(BF16).astype(F32)
    tmap[1, 1 : NP + 1, TOP : TOP + L, :] = merged.reshape(NP, L, CJ)
    put_edges(1)
    halo_copies(1, "start")
    exchange("send", o_source, recvo, o_ss, o_rs)
    second = conv(1)
    result = tmap[1, 1 : NP + 1, TOP : TOP + L, :] + second.reshape(NP, L, CJ)
    for q in range(NP // 2):
        blocks = [result[2 * q + s].T.reshape(C, PATCH, L) for s in range(2)]
        o_ref[:, 2 * PATCH * q : 2 * PATCH * (q + 1), :] = jnp.concatenate(blocks, axis=1).astype(
            BF16
        )
    halo_copies(1, "send")


def per_device(
    R, NC, pair_map, conv_in, embed_weight, qkv_weight, key_bias, out_weight, unpatch, conv_out
):
    NP = pair_map.shape[1] // PATCH
    L = pair_map.shape[2]
    PR = L // PATCH
    CJ = C * PATCH
    groups = NP * (D // LANES)
    vmem = pl.BlockSpec(memory_space=pltpu.VMEM)
    hbm = pl.BlockSpec(memory_space=pl.ANY)
    dma = pltpu.SemaphoreType.DMA
    return pl.pallas_call(
        functools.partial(trunk_kernel, R, NC),
        out_shape=jax.ShapeDtypeStruct(pair_map.shape, BF16),
        in_specs=[vmem] * 4 + [hbm] * 4,
        out_specs=vmem,
        scratch_shapes=[
            pltpu.VMEM((2, NP + 2, L + 2 * TOP, CJ), F32),
            pltpu.VMEM((2, NP * L, LANES), F32),
            pltpu.VMEM((2, 2, NP, CJ), F32),
            pltpu.VMEM((2, 2, 3, NP, CJ), F32),
            pltpu.VMEM((2, CJ * PATCH, LANES), F32),
            pltpu.VMEM(embed_weight.shape, BF16),
            pltpu.VMEM(qkv_weight.shape, BF16),
            pltpu.VMEM(out_weight.shape, BF16),
            pltpu.VMEM(unpatch.shape, BF16),
            pltpu.VMEM((PATCH, CJ, D), BF16),
            pltpu.VMEM((PATCH, CJ, D), BF16),
            pltpu.VMEM((2, 3, 2 * CJ, CJ), BF16),
            pltpu.VMEM((groups, PR, 3 * LANES), BF16),
            pltpu.VMEM((R, PR, 3 * LANES), BF16),
            pltpu.VMEM((NP, PR, LANES), BF16),
            pltpu.VMEM((R, PR, LANES), BF16),
            pltpu.VMEM((R, PR, LANES), BF16),
            pltpu.VMEM((R, PR, LANES), BF16),
            dma((4,)),
            dma((2, 2, 3)),
            dma((2, 2, 3)),
            dma((2, 2)),
            dma((2, 2)),
            dma((R,)),
            dma((R,)),
            dma((R,)),
            dma((R,)),
            dma((R,)),
            dma((R,)),
        ],
        compiler_params=pltpu.CompilerParams(
            collective_id=0, has_side_effects=True, vmem_limit_bytes=56 * 1024 * 1024
        ),
    )(
        pair_map,
        key_bias,
        conv_in,
        conv_out,
        embed_weight,
        qkv_weight,
        out_weight,
        unpatch,
    )


def solution(mesh):
    placed = (P(None, "cols", "rows"), P(), P(), P(), P("rows", "cols", None), P(), P(), P())
    return jax.shard_map(
        functools.partial(per_device, mesh.shape["rows"], mesh.shape["cols"]),
        mesh=mesh,
        in_specs=placed,
        out_specs=P(None, "cols", "rows"),
        check_vma=False,
    )
```

```python
import functools

import jax
import jax.numpy as jnp
from jax import lax
from jax.experimental import pallas as pl
from jax.experimental.pallas import tpu as pltpu
from jax.sharding import PartitionSpec as P

C = 32
PATCH = 8
D = 256
HEADS = 8
HEAD_DIM = 32
LANES = 128
EPSILON = 1e-05
F32 = jnp.float32
BF16 = jnp.bfloat16
MESH = pl.DeviceIdType.MESH
NT = (((1,), (1,)), ((), ()))
TOP = 8


def dot(a, b):
    return jnp.dot(a, b, preferred_element_type=F32)


def dot_nt(a, b):
    return lax.dot_general(a, b, NT, preferred_element_type=F32)


def iota(shape, dim):
    return lax.broadcasted_iota(jnp.int32, shape, dim)


def trunk_kernel(
    R,
    NC,
    x_ref,
    kb_ref,
    cin_ref,
    cout_ref,
    embed_hbm,
    qkv_hbm,
    outw_hbm,
    unp_hbm,
    o_ref,
    tmap,
    mixed,
    edges,
    halo,
    wide,
    embed_v,
    qkv_v,
    outw_v,
    unp_v,
    embed_i,
    unp_i,
    taps,
    sendq,
    recvq,
    sendb,
    recvb,
    sendo,
    recvo,
    load_sem,
    halo_ss,
    halo_rs,
    col_ss,
    col_rs,
    q_ss,
    q_rs,
    b_ss,
    b_rs,
    o_ss,
    o_rs,
    met,
):
    row = lax.axis_index("rows")
    col = lax.axis_index("cols")
    NP = x_ref.shape[1] // PATCH
    L = x_ref.shape[2]
    PR = L // PATCH
    CJ = C * PATCH
    groups = NP * (D // LANES)
    split = R // groups
    group_heads = LANES // HEAD_DIM
    my_heads = group_heads // split
    keys = R * PR
    bits = R.bit_length() - 1

    loads = [
        pltpu.make_async_copy(src, dst, load_sem.at[n])
        for n, (src, dst) in enumerate(
            ((embed_hbm, embed_v), (qkv_hbm, qkv_v), (outw_hbm, outw_v), (unp_hbm, unp_v))
        )
    ]
    for copy in loads:
        copy.start()

    row_ok = {-1: row > 0, 1: row < R - 1}
    col_ok = {-1: col > 0, 0: col >= 0, 1: col < NC - 1}
    barrier = pltpu.get_barrier_semaphore()

    def greet(peer_row, peer_col):
        pl.semaphore_signal(
            barrier,
            inc=1,
            device_id={"rows": peer_row, "cols": peer_col},
            device_id_type=MESH,
        )

    def partner(k):
        low = lax.rem(row // 2**k, 2)
        return row + (1 - 2 * low) * 2**k

    for k in range(bits):
        greet(partner(k), col)
    expected = bits
    for dr in (-1, 1):
        expected = expected + row_ok[dr].astype(jnp.int32)

        @pl.when(row_ok[dr])
        def _():
            greet(row + dr, col)

    for dc in (-1, 1):
        for dr in (-1, 0, 1):
            ok = col_ok[dc] if dr == 0 else jnp.logical_and(col_ok[dc], row_ok[dr])
            expected = expected + ok.astype(jnp.int32)

            @pl.when(ok)
            def _():
                greet(row + dr, col + dc)

    def put_edges(phase):
        for p in range(NP):
            edges[phase, 0, p : p + 1, :] = tmap[phase, p + 1, TOP + L - 1 : TOP + L, :]
            edges[phase, 1, p : p + 1, :] = tmap[phase, p + 1, TOP : TOP + 1, :]

    for q in range(NP // 2):
        pair = x_ref[:, 2 * PATCH * q : 2 * PATCH * (q + 1), :].astype(F32)
        for s in range(2):
            block = pair[:, PATCH * s : PATCH * (s + 1), :].reshape(CJ, L)
            tmap[0, 1 + 2 * q + s, TOP : TOP + L, :] = block.T
    put_edges(0)

    same = (iota((PR, PR), 0) == iota((PR, PR), 1)).astype(F32).astype(BF16)
    bias = dot_nt(same, kb_ref[...].astype(F32).reshape(NP * HEADS, PR).astype(BF16))
    pad = jnp.zeros((PR, LANES - NP * HEADS), F32)
    sendb[...] = jnp.concatenate([bias, pad], axis=1).astype(BF16)

    for phase in range(2):
        for way, dr in ((0, -1), (1, 1)):
            for slot in range(3):
                missing = jnp.logical_not(jnp.logical_and(row_ok[dr], col_ok[slot - 1]))

                @pl.when(missing)
                def _():
                    halo[phase, way, slot] = jnp.zeros((NP, CJ), F32)

        for side, dc in ((0, -1), (1, 1)):

            @pl.when(jnp.logical_not(col_ok[dc]))
            def _():
                tmap[phase, side * (NP + 1), TOP : TOP + L, :] = jnp.zeros((L, CJ), F32)

    pl.semaphore_wait(barrier, expected)

    def halo_copies(phase, act):
        for side, dc in ((0, 1), (1, -1)):
            copy = pltpu.make_async_remote_copy(
                src_ref=tmap.at[phase, NP if side == 0 else 1, pl.ds(TOP, L)],
                dst_ref=tmap.at[phase, 0 if side == 0 else NP + 1, pl.ds(TOP, L)],
                send_sem=col_ss.at[phase, side],
                recv_sem=col_rs.at[phase, side],
                device_id={"rows": row, "cols": col + (-dc if act == "recv" else dc)},
                device_id_type=MESH,
            )
            ok = col_ok[-dc] if act == "recv" else col_ok[dc]

            @pl.when(ok)
            def _():
                if act == "start":
                    copy.start()
                elif act == "send":
                    copy.wait_send()
                else:
                    copy.wait_recv()

        for way, dr in ((0, 1), (1, -1)):
            for slot in range(3):
                dc = slot - 1
                if act == "recv":
                    ok = jnp.logical_and(row_ok[-dr], col_ok[dc])
                    peer = {"rows": row - dr, "cols": col + dc}
                else:
                    ok = jnp.logical_and(row_ok[dr], col_ok[-dc])
                    peer = {"rows": row + dr, "cols": col - dc}
                copy = pltpu.make_async_remote_copy(
                    src_ref=edges.at[phase, way],
                    dst_ref=halo.at[phase, way, slot],
                    send_sem=halo_ss.at[phase, way, slot],
                    recv_sem=halo_rs.at[phase, way, slot],
                    device_id=peer,
                    device_id_type=MESH,
                )

                @pl.when(ok)
                def _():
                    if act == "start":
                        copy.start()
                    elif act == "send":
                        copy.wait_send()
                    else:
                        copy.wait_recv()

    def exchange(act, source, target, send_sem, recv_sem):
        def step(d, carry):
            peer = lax.rem(row + d, R)
            copy = pltpu.make_async_remote_copy(
                src_ref=source(peer),
                dst_ref=target.at[peer if act == "recv" else row],
                send_sem=send_sem.at[peer],
                recv_sem=recv_sem.at[peer if act == "recv" else row],
                device_id={"rows": peer, "cols": col},
                device_id_type=MESH,
            )
            if act == "start":
                copy.start()
            elif act == "send":
                copy.wait_send()
            else:
                copy.wait_recv()
            return carry

        lax.fori_loop(1, R, step, 0)

    halo_copies(0, "start")

    def tell(k):
        pl.semaphore_signal(
            met.at[k], inc=1, device_id={"rows": partner(k), "cols": col}, device_id_type=MESH
        )

    def hear(k):
        pl.semaphore_wait(met.at[k], 1)

    tell(0)

    spread = (iota((CJ, C), 0) // PATCH == iota((CJ, C), 1)).astype(F32).astype(BF16)
    both = jnp.concatenate(
        [dot(spread, cin_ref[...]).astype(BF16), dot(spread, cout_ref[...]).astype(BF16)], axis=0
    )
    in_place = iota((CJ, 2 * CJ), 0) % PATCH
    out_place = iota((CJ, 2 * CJ), 1) % PATCH
    channel = iota((CJ, 9 * C), 0) // PATCH
    tap = iota((CJ, 9 * C), 1)
    for b in range(3):
        centre = jnp.zeros((CJ, 2 * CJ), F32)
        rim = jnp.zeros((CJ, 2 * CJ), F32)
        for a in range(3):
            pick = (tap == channel + (3 * a + b) * C).astype(F32).astype(BF16)
            full = dot_nt(pick, both)
            centre = jnp.where(in_place == out_place + (a - 1), full, centre)
            if a == 0:
                rim = jnp.where(in_place == out_place + (PATCH - 1), full, rim)
            if a == 2:
                rim = jnp.where(in_place == out_place - (PATCH - 1), full, rim)
        for n in range(2):
            taps[n, b, 0:CJ, :] = centre[:, n * CJ : (n + 1) * CJ].astype(BF16)
            taps[n, b, CJ : 2 * CJ, :] = rim[:, n * CJ : (n + 1) * CJ].astype(BF16)
        if b < 2 and b + 1 < bits:
            hear(b)
            tell(b + 1)

    loads[0].wait()
    for half in range(2):
        wide[half] = embed_v[:, half * LANES : (half + 1) * LANES].astype(F32)
    for i in range(PATCH):
        for half in range(2):
            embed_i[i, :, half * LANES : (half + 1) * LANES] = wide[
                half, pl.ds(i, CJ, stride=PATCH), :
            ].astype(BF16)

    if bits > 3:
        hear(2)
        tell(3)
    lane_place = iota((1, 1, CJ), 2) % PATCH

    def conv(phase):
        halo_copies(phase, "recv")
        for way, place in ((0, TOP - 1), (1, TOP + L)):
            for p in range(NP):
                tmap[phase, p + 1, place : place + 1, :] = halo[phase, way, 1, p : p + 1, :]
            tmap[phase, 0, place : place + 1, :] = halo[phase, way, 0, NP - 1 : NP, :]
            tmap[phase, NP + 1, place : place + 1, :] = halo[phase, way, 2, 0:1, :]
        total = None
        for b in range(3):
            cells = tmap[phase, :, TOP - 1 + b : TOP - 1 + b + L, :]
            centre = cells[1 : NP + 1].reshape(NP * L, CJ).astype(BF16)
            rim = jnp.where(
                lane_place == PATCH - 1,
                cells[0:NP],
                jnp.where(lane_place == 0, cells[2 : NP + 2], 0.0),
            )
            rim = rim.reshape(NP * L, CJ).astype(BF16)
            part = dot(centre, taps[phase, b, 0:CJ, :]) + dot(rim, taps[phase, b, CJ : 2 * CJ, :])
            total = part if total is None else total + part
        return total

    first = conv(0)
    base = tmap[0, 1 : NP + 1, TOP : TOP + L, :].reshape(NP * L, CJ)
    mix = (base + first / (1.0 + jnp.exp(-first))).astype(BF16).astype(F32)
    for half in range(2):
        mixed[half] = mix[:, half * LANES : (half + 1) * LANES]

    for k in range(3 if bits > 3 else bits - 1, bits):
        hear(k)
        if k + 1 < bits:
            tell(k + 1)
    bias_source = lambda peer: sendb
    exchange("start", bias_source, recvb, b_ss, b_rs)
    recvb[row] = sendb[...]

    total = None
    for i in range(PATCH):
        for half in range(2):
            cells = mixed[half, pl.ds(i, NP * PR, stride=PATCH), :].astype(BF16)
            part = dot(cells, embed_i[i, half * LANES : (half + 1) * LANES, :])
            total = part if total is None else total + part
    tokens = total.astype(BF16).astype(F32)
    mean = jnp.mean(tokens, axis=1, keepdims=True)
    centred = tokens - mean
    var = jnp.mean(centred * centred, axis=1, keepdims=True)
    normed = (centred * lax.rsqrt(var + EPSILON)).astype(BF16)
    loads[1].wait()
    projected = dot(normed, qkv_v[...]).astype(BF16)
    for g in range(D // LANES):
        for kind in range(3):
            start = kind * D + g * LANES
            part = projected[:, start : start + LANES].reshape(NP, PR, LANES)
            for p in range(NP):
                sendq[p * (D // LANES) + g, :, kind * LANES : (kind + 1) * LANES] = part[p]
    q_source = lambda peer: sendq.at[peer // split]
    exchange("start", q_source, recvq, q_ss, q_rs)
    recvq[row] = sendq[row // split]

    loads[3].wait()
    for k in range(PATCH):
        block = unp_v[:, k * CJ : (k + 1) * CJ].astype(F32).T
        for half in range(2):
            wide[half, k * CJ : (k + 1) * CJ, :] = block[:, half * LANES : (half + 1) * LANES]
    for i in range(PATCH):
        for half in range(2):
            unp_i[i, :, half * LANES : (half + 1) * LANES] = wide[
                half, pl.ds(i, CJ, stride=PATCH), :
            ].astype(BF16)

    exchange("recv", bias_source, recvb, b_ss, b_rs)
    first_head = lax.rem(row, split) * my_heads
    first_global = (row // split) * group_heads + first_head
    pick = (iota((16, LANES), 1) == iota((16, LANES), 0) + first_global).astype(F32).astype(BF16)
    key_shift = dot_nt(pick, recvb[...].reshape(keys, LANES))
    exchange("recv", q_source, recvq, q_ss, q_rs)
    queries = recvq[:, :, 0:LANES].reshape(keys, LANES).astype(F32)
    key_rows = recvq[:, :, LANES : 2 * LANES].reshape(keys, LANES)
    values = recvq[:, :, 2 * LANES : 3 * LANES].reshape(keys, LANES).astype(F32)
    lane_head = iota((1, LANES), 1) // HEAD_DIM
    total = None
    for k in range(my_heads):
        mine = lane_head == first_head + k
        query = jnp.where(mine, queries, 0.0).astype(BF16)
        scores = dot_nt(query, key_rows) * (HEAD_DIM**-0.5) + key_shift[k : k + 1, :]
        weights = jnp.exp(scores - jnp.max(scores, axis=1, keepdims=True))
        soft = (weights / jnp.sum(weights, axis=1, keepdims=True)).astype(BF16)
        part = dot(soft, jnp.where(mine, values, 0.0).astype(BF16))
        total = part if total is None else total + part
    sendo[...] = total.astype(BF16).reshape(R, PR, LANES)
    o_source = lambda peer: sendo.at[peer]
    exchange("start", o_source, recvo, o_ss, o_rs)
    recvo[row] = sendo[row]
    loads[2].wait()
    exchange("send", bias_source, recvb, b_ss, b_rs)
    exchange("send", q_source, recvq, q_ss, q_rs)
    halo_copies(0, "send")
    exchange("recv", o_source, recvo, o_ss, o_rs)

    back = recvo[...].reshape(NP, D // LANES, split, PR, LANES)
    sides = []
    for g in range(D // LANES):
        share = back[:, g, 0]
        for s in range(1, split):
            share = share + back[:, g, s]
        sides.append(share.reshape(NP * PR, LANES))
    attended = jnp.concatenate(sides, axis=1)
    updated = (tokens + dot(attended, outw_v[...])).astype(BF16)
    for i in range(PATCH):
        expanded = dot_nt(updated, unp_i[i])
        for half in range(2):
            wide[half, pl.ds(i, NP * PR, stride=PATCH), :] = expanded[
                :, half * LANES : (half + 1) * LANES
            ]
    merged = jnp.concatenate(
        [mixed[half] + wide[half, 0 : NP * L, :] for half in range(2)], axis=1
    )
    merged = merged.astype(BF16).astype(F32)
    tmap[1, 1 : NP + 1, TOP : TOP + L, :] = merged.reshape(NP, L, CJ)
    put_edges(1)
    halo_copies(1, "start")
    exchange("send", o_source, recvo, o_ss, o_rs)
    second = conv(1)
    result = tmap[1, 1 : NP + 1, TOP : TOP + L, :] + second.reshape(NP, L, CJ)
    for q in range(NP // 2):
        blocks = [result[2 * q + s].T.reshape(C, PATCH, L) for s in range(2)]
        o_ref[:, 2 * PATCH * q : 2 * PATCH * (q + 1), :] = jnp.concatenate(blocks, axis=1).astype(
            BF16
        )
    halo_copies(1, "send")


def per_device(
    R, NC, pair_map, conv_in, embed_weight, qkv_weight, key_bias, out_weight, unpatch, conv_out
):
    NP = pair_map.shape[1] // PATCH
    L = pair_map.shape[2]
    PR = L // PATCH
    CJ = C * PATCH
    groups = NP * (D // LANES)
    vmem = pl.BlockSpec(memory_space=pltpu.VMEM)
    hbm = pl.BlockSpec(memory_space=pl.ANY)
    dma = pltpu.SemaphoreType.DMA
    return pl.pallas_call(
        functools.partial(trunk_kernel, R, NC),
        out_shape=jax.ShapeDtypeStruct(pair_map.shape, BF16),
        in_specs=[vmem] * 4 + [hbm] * 4,
        out_specs=vmem,
        scratch_shapes=[
            pltpu.VMEM((2, NP + 2, L + 2 * TOP, CJ), F32),
            pltpu.VMEM((2, NP * L, LANES), F32),
            pltpu.VMEM((2, 2, NP, CJ), F32),
            pltpu.VMEM((2, 2, 3, NP, CJ), F32),
            pltpu.VMEM((2, CJ * PATCH, LANES), F32),
            pltpu.VMEM(embed_weight.shape, BF16),
            pltpu.VMEM(qkv_weight.shape, BF16),
            pltpu.VMEM(out_weight.shape, BF16),
            pltpu.VMEM(unpatch.shape, BF16),
            pltpu.VMEM((PATCH, CJ, D), BF16),
            pltpu.VMEM((PATCH, CJ, D), BF16),
            pltpu.VMEM((2, 3, 2 * CJ, CJ), BF16),
            pltpu.VMEM((groups, PR, 3 * LANES), BF16),
            pltpu.VMEM((R, PR, 3 * LANES), BF16),
            pltpu.VMEM((PR, LANES), BF16),
            pltpu.VMEM((R, PR, LANES), BF16),
            pltpu.VMEM((R, PR, LANES), BF16),
            pltpu.VMEM((R, PR, LANES), BF16),
            dma((4,)),
            dma((2, 2, 3)),
            dma((2, 2, 3)),
            dma((2, 2)),
            dma((2, 2)),
            dma((R,)),
            dma((R,)),
            dma((R,)),
            dma((R,)),
            dma((R,)),
            dma((R,)),
            pltpu.SemaphoreType.REGULAR((R.bit_length() - 1,)),
        ],
        compiler_params=pltpu.CompilerParams(
            collective_id=0, has_side_effects=True, vmem_limit_bytes=56 * 1024 * 1024
        ),
    )(
        pair_map,
        key_bias.transpose(1, 2, 0),
        conv_in,
        conv_out,
        embed_weight,
        qkv_weight,
        out_weight,
        unpatch,
    )


def solution(mesh):
    placed = (P(None, "cols", "rows"), P(), P(), P(), P("rows", "cols", None), P(), P(), P())
    return jax.shard_map(
        functools.partial(per_device, mesh.shape["rows"], mesh.shape["cols"]),
        mesh=mesh,
        in_specs=placed,
        out_specs=P(None, "cols", "rows"),
        check_vma=False,
    )
```

```python
import functools

import jax
import jax.numpy as jnp
from jax import lax
from jax.experimental import pallas as pl
from jax.experimental.pallas import tpu as pltpu
from jax.sharding import PartitionSpec as P

C = 32
PATCH = 8
D = 256
HEADS = 8
HEAD_DIM = 32
LANES = 128
EPSILON = 1e-05
F32 = jnp.float32
BF16 = jnp.bfloat16
MESH = pl.DeviceIdType.MESH
NT = (((1,), (1,)), ((), ()))
TOP = 8


def dot(a, b):
    return jnp.dot(a, b, preferred_element_type=F32)


def dot_nt(a, b):
    return lax.dot_general(a, b, NT, preferred_element_type=F32)


def iota(shape, dim):
    return lax.broadcasted_iota(jnp.int32, shape, dim)


def trunk_kernel(
    R,
    NC,
    x_ref,
    kb_ref,
    cin_ref,
    cout_ref,
    embed_hbm,
    qkv_hbm,
    outw_hbm,
    unp_hbm,
    o_ref,
    tmap,
    mixed,
    edges,
    halo,
    wide,
    embed_v,
    qkv_v,
    outw_v,
    unp_v,
    embed_i,
    unp_i,
    taps,
    sendq,
    recvq,
    sendo,
    recvo,
    load_sem,
    halo_ss,
    halo_rs,
    col_ss,
    col_rs,
    q_ss,
    q_rs,
    o_ss,
    o_rs,
    met,
):
    row = lax.axis_index("rows")
    col = lax.axis_index("cols")
    NP = x_ref.shape[1] // PATCH
    L = x_ref.shape[2]
    PR = L // PATCH
    CJ = C * PATCH
    groups = NP * (D // LANES)
    split = R // groups
    group_heads = LANES // HEAD_DIM
    my_heads = group_heads // split
    keys = R * PR
    bits = R.bit_length() - 1

    loads = [
        pltpu.make_async_copy(src, dst, load_sem.at[n])
        for n, (src, dst) in enumerate(
            ((embed_hbm, embed_v), (qkv_hbm, qkv_v), (outw_hbm, outw_v), (unp_hbm, unp_v))
        )
    ]
    for copy in loads:
        copy.start()

    row_ok = {-1: row > 0, 1: row < R - 1}
    col_ok = {-1: col > 0, 0: col >= 0, 1: col < NC - 1}
    barrier = pltpu.get_barrier_semaphore()

    def greet(peer_row, peer_col):
        pl.semaphore_signal(
            barrier,
            inc=1,
            device_id={"rows": peer_row, "cols": peer_col},
            device_id_type=MESH,
        )

    def partner(k):
        low = lax.rem(row // 2**k, 2)
        return row + (1 - 2 * low) * 2**k

    flips = [partner(k) - row for k in range(bits)]
    for k in range(bits):
        greet(partner(k), col)
    expected = bits
    for dr in (-1, 1):
        expected = expected + row_ok[dr].astype(jnp.int32)

        @pl.when(row_ok[dr])
        def _():
            greet(row + dr, col)

    for dc in (-1, 1):
        for dr in (-1, 0, 1):
            ok = col_ok[dc] if dr == 0 else jnp.logical_and(col_ok[dc], row_ok[dr])
            expected = expected + ok.astype(jnp.int32)

            @pl.when(ok)
            def _():
                greet(row + dr, col + dc)

    def put_edges(phase):
        for p in range(NP):
            edges[phase, 0, p : p + 1, :] = tmap[phase, p + 1, TOP + L - 1 : TOP + L, :]
            edges[phase, 1, p : p + 1, :] = tmap[phase, p + 1, TOP : TOP + 1, :]

    for q in range(NP // 2):
        pair = x_ref[:, 2 * PATCH * q : 2 * PATCH * (q + 1), :].astype(F32)
        for s in range(2):
            block = pair[:, PATCH * s : PATCH * (s + 1), :].reshape(CJ, L)
            tmap[0, 1 + 2 * q + s, TOP : TOP + L, :] = block.T
    put_edges(0)

    same = (iota((PR, PR), 0) == iota((PR, PR), 1)).astype(F32).astype(BF16)
    bias = dot_nt(same, kb_ref[...].astype(F32).reshape(NP * HEADS, PR).astype(BF16))
    pad = jnp.zeros((PR, LANES - NP * HEADS), F32)
    bias = jnp.concatenate([bias, pad], axis=1).astype(BF16)
    for g in range(groups):
        sendq[g, :, 3 * LANES : 4 * LANES] = bias

    for phase in range(2):
        for way, dr in ((0, -1), (1, 1)):
            for slot in range(3):
                missing = jnp.logical_not(jnp.logical_and(row_ok[dr], col_ok[slot - 1]))

                @pl.when(missing)
                def _():
                    halo[phase, way, slot] = jnp.zeros((NP, CJ), F32)

        for side, dc in ((0, -1), (1, 1)):

            @pl.when(jnp.logical_not(col_ok[dc]))
            def _():
                tmap[phase, side * (NP + 1), TOP : TOP + L, :] = jnp.zeros((L, CJ), F32)

    def banded(n, weight):
        spread = (iota((CJ, C), 0) // PATCH == iota((CJ, C), 1)).astype(F32).astype(BF16)
        wide_weight = dot(spread, weight).astype(BF16)
        shift = iota((CJ, CJ), 0) % PATCH - iota((CJ, CJ), 1) % PATCH
        ahead = iota((CJ, 9 * C), 1) - iota((CJ, 9 * C), 0) // PATCH
        for b in range(3):
            centre = jnp.zeros((CJ, CJ), F32)
            rim = jnp.zeros((CJ, CJ), F32)
            for a in range(3):
                pick = (ahead == (3 * a + b) * C).astype(F32).astype(BF16)
                full = dot_nt(pick, wide_weight)
                centre = jnp.where(shift == a - 1, full, centre)
                if a == 0:
                    rim = jnp.where(shift == PATCH - 1, full, rim)
                if a == 2:
                    rim = jnp.where(shift == 1 - PATCH, full, rim)
            taps[n, b, 0:CJ, :] = centre.astype(BF16)
            taps[n, b, CJ : 2 * CJ, :] = rim.astype(BF16)

    banded(0, cin_ref[...])

    pl.semaphore_wait(barrier, expected)

    def halo_copies(phase, act):
        for side, dc in ((0, 1), (1, -1)):
            copy = pltpu.make_async_remote_copy(
                src_ref=tmap.at[phase, NP if side == 0 else 1, pl.ds(TOP, L)],
                dst_ref=tmap.at[phase, 0 if side == 0 else NP + 1, pl.ds(TOP, L)],
                send_sem=col_ss.at[phase, side],
                recv_sem=col_rs.at[phase, side],
                device_id={"rows": row, "cols": col + (-dc if act == "recv" else dc)},
                device_id_type=MESH,
            )
            ok = col_ok[-dc] if act == "recv" else col_ok[dc]

            @pl.when(ok)
            def _():
                if act == "start":
                    copy.start()
                elif act == "send":
                    copy.wait_send()
                else:
                    copy.wait_recv()

        for way, dr in ((0, 1), (1, -1)):
            for slot in range(3):
                dc = slot - 1
                if act == "recv":
                    ok = jnp.logical_and(row_ok[-dr], col_ok[dc])
                    peer = {"rows": row - dr, "cols": col + dc}
                else:
                    ok = jnp.logical_and(row_ok[dr], col_ok[-dc])
                    peer = {"rows": row + dr, "cols": col - dc}
                copy = pltpu.make_async_remote_copy(
                    src_ref=edges.at[phase, way],
                    dst_ref=halo.at[phase, way, slot],
                    send_sem=halo_ss.at[phase, way, slot],
                    recv_sem=halo_rs.at[phase, way, slot],
                    device_id=peer,
                    device_id_type=MESH,
                )

                @pl.when(ok)
                def _():
                    if act == "start":
                        copy.start()
                    elif act == "send":
                        copy.wait_send()
                    else:
                        copy.wait_recv()

    def exchange(act, source, target, send_sem, recv_sem):
        for d in range(R - 1, 0, -1):
            peer = row
            for k in range(bits):
                if d // 2**k % 2:
                    peer = peer + flips[k]
            copy = pltpu.make_async_remote_copy(
                src_ref=source(peer),
                dst_ref=target.at[peer if act == "recv" else row],
                send_sem=send_sem.at[peer],
                recv_sem=recv_sem.at[peer if act == "recv" else row],
                device_id={"rows": peer, "cols": col},
                device_id_type=MESH,
            )
            if act == "start":
                copy.start()
            elif act == "send":
                copy.wait_send()
            else:
                copy.wait_recv()

    halo_copies(0, "start")

    def tell(k):
        pl.semaphore_signal(
            met.at[k], inc=1, device_id={"rows": partner(k), "cols": col}, device_id_type=MESH
        )

    def hear(k):
        pl.semaphore_wait(met.at[k], 1)

    tell(0)

    loads[0].wait()
    for half in range(2):
        wide[half] = embed_v[:, half * LANES : (half + 1) * LANES].astype(F32)
    for i in range(PATCH):
        for half in range(2):
            embed_i[i, :, half * LANES : (half + 1) * LANES] = wide[
                half, pl.ds(i, CJ, stride=PATCH), :
            ].astype(BF16)
        if i in (1, 4) and i // 3 + 1 < bits:
            hear(i // 3)
            tell(i // 3 + 1)

    if bits > 3:
        hear(2)
        tell(3)
    lane_place = iota((1, 1, CJ), 2) % PATCH

    def conv(phase):
        halo_copies(phase, "recv")
        for way, place in ((0, TOP - 1), (1, TOP + L)):
            for p in range(NP):
                tmap[phase, p + 1, place : place + 1, :] = halo[phase, way, 1, p : p + 1, :]
            tmap[phase, 0, place : place + 1, :] = halo[phase, way, 0, NP - 1 : NP, :]
            tmap[phase, NP + 1, place : place + 1, :] = halo[phase, way, 2, 0:1, :]
        total = None
        for b in range(3):
            cells = tmap[phase, :, TOP - 1 + b : TOP - 1 + b + L, :]
            centre = cells[1 : NP + 1].reshape(NP * L, CJ).astype(BF16)
            rim = jnp.where(
                lane_place == PATCH - 1,
                cells[0:NP],
                jnp.where(lane_place == 0, cells[2 : NP + 2], 0.0),
            )
            rim = rim.reshape(NP * L, CJ).astype(BF16)
            part = dot(centre, taps[phase, b, 0:CJ, :]) + dot(rim, taps[phase, b, CJ : 2 * CJ, :])
            total = part if total is None else total + part
        return total

    first = conv(0)
    base = tmap[0, 1 : NP + 1, TOP : TOP + L, :].reshape(NP * L, CJ)
    mix = (base + first / (1.0 + jnp.exp(-first))).astype(BF16).astype(F32)
    for half in range(2):
        mixed[half] = mix[:, half * LANES : (half + 1) * LANES]

    for k in range(3 if bits > 3 else bits - 1, bits):
        hear(k)
        if k + 1 < bits:
            tell(k + 1)

    total = None
    for i in range(PATCH):
        for half in range(2):
            cells = mixed[half, pl.ds(i, NP * PR, stride=PATCH), :].astype(BF16)
            part = dot(cells, embed_i[i, half * LANES : (half + 1) * LANES, :])
            total = part if total is None else total + part
    tokens = total.astype(BF16).astype(F32)
    mean = jnp.mean(tokens, axis=1, keepdims=True)
    centred = tokens - mean
    var = jnp.mean(centred * centred, axis=1, keepdims=True)
    normed = (centred * lax.rsqrt(var + EPSILON)).astype(BF16)
    loads[1].wait()
    projected = dot(normed, qkv_v[...]).astype(BF16)
    for g in range(D // LANES):
        for kind in range(3):
            start = kind * D + g * LANES
            part = projected[:, start : start + LANES].reshape(NP, PR, LANES)
            for p in range(NP):
                sendq[p * (D // LANES) + g, :, kind * LANES : (kind + 1) * LANES] = part[p]
    q_source = lambda peer: sendq.at[peer // split]
    exchange("start", q_source, recvq, q_ss, q_rs)
    recvq[row] = sendq[row // split]

    loads[3].wait()
    for k in range(PATCH):
        block = unp_v[:, k * CJ : (k + 1) * CJ].astype(F32).T
        for half in range(2):
            wide[half, k * CJ : (k + 1) * CJ, :] = block[:, half * LANES : (half + 1) * LANES]
    for i in range(PATCH):
        for half in range(2):
            unp_i[i, :, half * LANES : (half + 1) * LANES] = wide[
                half, pl.ds(i, CJ, stride=PATCH), :
            ].astype(BF16)

    banded(1, cout_ref[...])
    exchange("recv", q_source, recvq, q_ss, q_rs)
    first_head = lax.rem(row, split) * my_heads
    first_global = (row // split) * group_heads + first_head
    pick = (iota((16, LANES), 1) == iota((16, LANES), 0) + first_global).astype(F32).astype(BF16)
    key_shift = dot_nt(pick, recvq[:, :, 3 * LANES : 4 * LANES].reshape(keys, LANES))
    queries = recvq[:, :, 0:LANES].reshape(keys, LANES).astype(F32)
    key_rows = recvq[:, :, LANES : 2 * LANES].reshape(keys, LANES)
    values = recvq[:, :, 2 * LANES : 3 * LANES].reshape(keys, LANES).astype(F32)
    lane_head = iota((1, LANES), 1) // HEAD_DIM
    total = None
    for k in range(my_heads):
        mine = lane_head == first_head + k
        query = jnp.where(mine, queries, 0.0).astype(BF16)
        scores = dot_nt(query, key_rows) * (HEAD_DIM**-0.5) + key_shift[k : k + 1, :]
        weights = jnp.exp(scores - jnp.max(scores, axis=1, keepdims=True))
        soft = (weights / jnp.sum(weights, axis=1, keepdims=True)).astype(BF16)
        part = dot(soft, jnp.where(mine, values, 0.0).astype(BF16))
        total = part if total is None else total + part
    sendo[...] = total.astype(BF16).reshape(R, PR, LANES)
    o_source = lambda peer: sendo.at[peer]
    exchange("start", o_source, recvo, o_ss, o_rs)
    recvo[row] = sendo[row]
    loads[2].wait()
    exchange("send", q_source, recvq, q_ss, q_rs)
    halo_copies(0, "send")
    exchange("recv", o_source, recvo, o_ss, o_rs)

    back = recvo[...].reshape(NP, D // LANES, split, PR, LANES)
    sides = []
    for g in range(D // LANES):
        share = back[:, g, 0]
        for s in range(1, split):
            share = share + back[:, g, s]
        sides.append(share.reshape(NP * PR, LANES))
    attended = jnp.concatenate(sides, axis=1)
    updated = (tokens + dot(attended, outw_v[...])).astype(BF16)
    for i in range(PATCH):
        expanded = dot_nt(updated, unp_i[i])
        for half in range(2):
            wide[half, pl.ds(i, NP * PR, stride=PATCH), :] = expanded[
                :, half * LANES : (half + 1) * LANES
            ]
    merged = jnp.concatenate(
        [mixed[half] + wide[half, 0 : NP * L, :] for half in range(2)], axis=1
    )
    merged = merged.astype(BF16).astype(F32)
    tmap[1, 1 : NP + 1, TOP : TOP + L, :] = merged.reshape(NP, L, CJ)
    put_edges(1)
    halo_copies(1, "start")
    exchange("send", o_source, recvo, o_ss, o_rs)
    second = conv(1)
    result = tmap[1, 1 : NP + 1, TOP : TOP + L, :] + second.reshape(NP, L, CJ)
    for q in range(NP // 2):
        blocks = [result[2 * q + s].T.reshape(C, PATCH, L) for s in range(2)]
        o_ref[:, 2 * PATCH * q : 2 * PATCH * (q + 1), :] = jnp.concatenate(blocks, axis=1).astype(
            BF16
        )
    halo_copies(1, "send")


def per_device(
    R, NC, pair_map, conv_in, embed_weight, qkv_weight, key_bias, out_weight, unpatch, conv_out
):
    NP = pair_map.shape[1] // PATCH
    L = pair_map.shape[2]
    PR = L // PATCH
    CJ = C * PATCH
    groups = NP * (D // LANES)
    vmem = pl.BlockSpec(memory_space=pltpu.VMEM)
    hbm = pl.BlockSpec(memory_space=pl.ANY)
    dma = pltpu.SemaphoreType.DMA
    return pl.pallas_call(
        functools.partial(trunk_kernel, R, NC),
        out_shape=jax.ShapeDtypeStruct(pair_map.shape, BF16),
        in_specs=[vmem] * 4 + [hbm] * 4,
        out_specs=vmem,
        scratch_shapes=[
            pltpu.VMEM((2, NP + 2, L + 2 * TOP, CJ), F32),
            pltpu.VMEM((2, NP * L, LANES), F32),
            pltpu.VMEM((2, 2, NP, CJ), F32),
            pltpu.VMEM((2, 2, 3, NP, CJ), F32),
            pltpu.VMEM((2, CJ * PATCH, LANES), F32),
            pltpu.VMEM(embed_weight.shape, BF16),
            pltpu.VMEM(qkv_weight.shape, BF16),
            pltpu.VMEM(out_weight.shape, BF16),
            pltpu.VMEM(unpatch.shape, BF16),
            pltpu.VMEM((PATCH, CJ, D), BF16),
            pltpu.VMEM((PATCH, CJ, D), BF16),
            pltpu.VMEM((2, 3, 2 * CJ, CJ), BF16),
            pltpu.VMEM((groups, PR, 4 * LANES), BF16),
            pltpu.VMEM((R, PR, 4 * LANES), BF16),
            pltpu.VMEM((R, PR, LANES), BF16),
            pltpu.VMEM((R, PR, LANES), BF16),
            dma((4,)),
            dma((2, 2, 3)),
            dma((2, 2, 3)),
            dma((2, 2)),
            dma((2, 2)),
            dma((R,)),
            dma((R,)),
            dma((R,)),
            dma((R,)),
            pltpu.SemaphoreType.REGULAR((R.bit_length() - 1,)),
        ],
        compiler_params=pltpu.CompilerParams(
            collective_id=0, has_side_effects=True, vmem_limit_bytes=56 * 1024 * 1024
        ),
    )(
        pair_map,
        key_bias.transpose(1, 2, 0),
        conv_in,
        conv_out,
        embed_weight,
        qkv_weight,
        out_weight,
        unpatch,
    )


def solution(mesh):
    placed = (P(None, "cols", "rows"), P(), P(), P(), P("rows", "cols", None), P(), P(), P())
    return jax.shard_map(
        functools.partial(per_device, mesh.shape["rows"], mesh.shape["cols"]),
        mesh=mesh,
        in_specs=placed,
        out_specs=P(None, "cols", "rows"),
        check_vma=False,
    )
```
